768 devices in a mesh: seq: 96 (over z, x, core), head: 8 (over y).
Axes of the slice: x: 4, y: 8, z: 12, core: 2. Of those that a mesh axis runs over, the one named last changes fastest.
Arguments:
- queries: bfloat16 [24576, 4096], P('seq', 'head'), may hold values from -6 to 6
- key_vectors: bfloat16 [24576, 4096], P('seq', 'head'), may hold values from -0.5 to 0.5
- value_vectors: bfloat16 [24576, 4096], P('seq', 'head'), may hold values from -60 to 60
- out_grad: bfloat16 [24576, 4096], P('seq', 'head'), may hold values from -9.5 to 9.5
- norm_gain: float32 [4096], P('head'), may hold values from 0.1 to 1.9
Outputs:
- grad_queries: bfloat16 [24576, 4096], P('seq', 'head')
- grad_keys: bfloat16 [24576, 4096], P('seq', 'head')
- grad_values: bfloat16 [24576, 4096], P('seq', 'head')
- grad_gain: float32 [4096], P('head')
The draws below stay inside these ranges and needn't reach their ends.
All inputs are finite; a program needn't handle non-finite values.
Results may differ from the reference program's by a relative error of at most 0.0049.
Values sent between devices are 32-bit elements; how exact they have to be, the bound alone decides.
A program may use at most 64 MiB of HBM per device.

```python
import math
import jax
import jax.numpy as jnp
from jax import lax

DH = 128
BLOCK = 128
HEADS = 32
DMODEL = 4096
TOKENS = 24576


def draw_value_vectors(key, part):
    first_key, second_key = jax.random.split(jax.random.fold_in(key, 11))
    base = jnp.clip(jax.random.normal(first_key, (TOKENS, DMODEL), jnp.float32), -6.0, 6.0)
    row_scale = jnp.exp(jax.random.uniform(second_key, (TOKENS, 1), jnp.float32, math.log(0.3), math.log(3.0)))
    head_place = (jnp.arange(DMODEL) // DH).astype(jnp.float32) / (HEADS - 1)
    column_scale = jnp.exp(head_place * 0.5 * math.log(10.0))
    return (base * row_scale * column_scale[None, :]).astype(jnp.bfloat16)


def draw_out_grad(key, part):
    first_key = jax.random.fold_in(key, 23)
    position = jnp.arange(TOKENS).astype(jnp.float32) / (TOKENS - 1)
    rising = 0.5 + position
    base = jnp.clip(jax.random.normal(first_key, (TOKENS, DMODEL), jnp.float32), -6.0, 6.0)
    return (base * rising[:, None]).astype(jnp.bfloat16)


def level_of(rng, dims, shards, low, high):
    loudness = 1.0
    for axis_at, blocks in shards:
        draws = jax.random.uniform(jax.random.fold_in(jax.random.fold_in(rng, 6), axis_at), (blocks,), jnp.float32, low / len(shards), high / len(shards))
        loudness = loudness * jnp.repeat(jnp.exp(draws), dims[axis_at] // blocks).reshape((-1,) + (1,) * (len(dims) - 1 - axis_at))
    return loudness


def scatter_about(key, dims, spread, reach, shards=(), kind=jnp.bfloat16):
    array = jax.random.normal(key, dims, jnp.float32) * spread
    if len(shards) > 0:
        array = level_of(key, dims, shards, -0.22, 0.18) * array
    return jnp.clip(array, min=-reach, max=reach).astype(kind)


def setup_inputs(seed: int = 0) -> dict:
    key_list = jax.random.split(jax.random.key(seed), 6)
    queries = scatter_about(key_list[0], (TOKENS, DMODEL), 1.0, 6.0, ((0, 96), (1, 8)))
    key_vectors = scatter_about(key_list[1], (TOKENS, DMODEL), DH ** -0.5, 0.5, ((0, 96), (1, 8)))
    value_vectors = draw_value_vectors(jax.random.fold_in(key_list[5], 71), 0)
    out_grad = draw_out_grad(jax.random.fold_in(key_list[5], 71), 0)
    norm_gain = jnp.clip(1.0 + 0.18 * jax.random.normal(key_list[4], (DMODEL,), jnp.float32), 0.1, 1.9)
    return dict(queries=queries, key_vectors=key_vectors, value_vectors=value_vectors, out_grad=out_grad, norm_gain=norm_gain)


epsilon = 1e-06

def causal_pairs():
    return jnp.arange(BLOCK)[:, None] >= jnp.arange(BLOCK)[None, :]

def head_forward(query_head, key_head, value_head):
    query_f32 = query_head.reshape(-1, BLOCK, DH).astype(jnp.float32)
    key_f32 = key_head.reshape(-1, BLOCK, DH).astype(jnp.float32)
    value_f32 = value_head.reshape(-1, BLOCK, DH).astype(jnp.float32)
    products = jnp.einsum('btd,bsd->bts', query_f32, key_f32)
    scores = jnp.where(causal_pairs()[None], products, 0.0).astype(jnp.bfloat16)
    key_value = jnp.einsum('bsd,bse->bde', key_f32, value_f32)
    running = jnp.cumsum(key_value, axis=0)
    states = jnp.concatenate([jnp.zeros_like(key_value[:1]), running[:-1]], axis=0)
    attention = jnp.einsum('bts,bse->bte', scores.astype(jnp.float32), value_f32)
    attention = attention + jnp.einsum('btd,bde->bte', query_f32, states, precision=lax.Precision.HIGHEST)
    return (scores, states, attention, query_f32, key_f32, value_f32)

def split_heads(matrix):
    return matrix.reshape(TOKENS, HEADS, DH).transpose(1, 0, 2)

def join_heads(stacked):
    return stacked.transpose(1, 0, 2).reshape(TOKENS, DMODEL)

def reference(queries, key_vectors, value_vectors, out_grad, norm_gain):
    query_heads = split_heads(queries)
    key_heads = split_heads(key_vectors)
    value_heads = split_heads(value_vectors)
    grad_heads = split_heads(out_grad)
    gain_heads = norm_gain.reshape(HEADS, DH)

    def first_pass(items):
        query_head, key_head, value_head, grad_head, gain_head = items
        attention = head_forward(query_head, key_head, value_head)[2].reshape(TOKENS, DH)
        square_sum = lax.optimization_barrier(jnp.sum(attention * attention, axis=1))
        weighted = lax.optimization_barrier(jnp.sum(gain_head[None, :] * grad_head.astype(jnp.float32) * attention, axis=1))
        return (square_sum, weighted)
    square_parts, weighted_parts = lax.map(first_pass, (query_heads, key_heads, value_heads, grad_heads, gain_heads))
    square_sum = lax.optimization_barrier(jnp.sum(square_parts, axis=0))
    weighted = lax.optimization_barrier(jnp.sum(weighted_parts, axis=0))
    inverse_rms = 1.0 / jnp.sqrt(square_sum / DMODEL + epsilon)

    def second_pass(items):
        query_head, key_head, value_head, grad_head, gain_head = items
        scores, states, attention, query_f32, key_f32, value_f32 = head_forward(query_head, key_head, value_head)
        attention = attention.reshape(TOKENS, DH)
        grad_f32 = grad_head.astype(jnp.float32)
        gain_part = lax.optimization_barrier(jnp.sum(grad_f32 * attention * inverse_rms[:, None], axis=0))
        grad_attention = gain_head[None, :] * grad_f32 * inverse_rms[:, None]
        grad_attention = grad_attention - attention * (inverse_rms ** 3 * weighted / DMODEL)[:, None]
        grad_attention = grad_attention.astype(jnp.bfloat16).reshape(-1, BLOCK, DH).astype(jnp.float32)
        products = jnp.einsum('bte,bse->bts', grad_attention, value_f32)
        grad_scores = jnp.where(causal_pairs()[None], products, 0.0).astype(jnp.bfloat16).astype(jnp.float32)
        query_grad = jnp.einsum('btd,bte->bde', query_f32, grad_attention)
        backward = jnp.cumsum(query_grad[::-1], axis=0)[::-1]
        later = jnp.concatenate([backward[1:], jnp.zeros_like(query_grad[:1])], axis=0)
        high = lax.Precision.HIGHEST
        grad_query = jnp.einsum('bts,bsd->btd', grad_scores, key_f32)
        grad_query = grad_query + jnp.einsum('bte,bde->btd', grad_attention, states, precision=high)
        grad_key = jnp.einsum('bts,btd->bsd', grad_scores, query_f32)
        grad_key = grad_key + jnp.einsum('bse,bde->bsd', value_f32, later, precision=high)
        grad_value = jnp.einsum('bts,bte->bse', scores.astype(jnp.float32), grad_attention)
        grad_value = grad_value + jnp.einsum('bsd,bde->bse', key_f32, later, precision=high)
        return (grad_query.reshape(TOKENS, DH).astype(jnp.bfloat16), grad_key.reshape(TOKENS, DH).astype(jnp.bfloat16), grad_value.reshape(TOKENS, DH).astype(jnp.bfloat16), gain_part)
    grad_query, grad_key, grad_value, gain_parts = lax.map(second_pass, (query_heads, key_heads, value_heads, grad_heads, gain_heads))
    return (join_heads(grad_query), join_heads(grad_key), join_heads(grad_value), gain_parts.reshape(DMODEL))
```

```python
import functools

import jax
import jax.numpy as jnp
from jax import lax
from jax.experimental import pallas as pl
from jax.experimental.pallas import tpu as pltpu
from jax.sharding import PartitionSpec as P

DH = 128
BLOCK = 128
PLANE = 8
NEAR = (1, 2, 3)
FAR = (4, 8)
EPSILON = 1e-06
MESH = pl.DeviceIdType.MESH
F32 = jnp.float32
BF16 = jnp.bfloat16


def dot(left, right, left_dim, right_dim):
    return lax.dot_general(
        left, right, (((left_dim,), (right_dim,)), ((), ())), preferred_element_type=F32
    )


def split(wide):
    high = wide.astype(BF16)
    low = (wide - high.astype(F32)).astype(BF16)
    return high, low


def dot_wide(left, wide, wide_dim):
    high, low = split(wide)
    return dot(left, high, 1, wide_dim) + dot(left, low, 1, wide_dim)


def kernel(
    z_count, y_count, head_count, block_count,
    q_ref, k_ref, v_ref, g_ref, gain_ref,
    gq_ref, gk_ref, gv_ref, gg_ref,
    inner, att, scores, grad_att, gk_part, gv_part, earlier, later,
    total_f, plane_f, step_f, near_f, window_f, far_f, stage_f,
    total_b, plane_b, step_b, near_b, window_b, far_b, stage_b,
    sums,
    fa_send, fa_recv, fb_send, fb_recv, fc_send, fc_recv,
    ba_send, ba_recv, bb_send, bb_recv, bc_send, bc_recv,
    h_send, h_recv,
):
    seq = lax.axis_index("seq")
    y = lax.axis_index("head")
    z = lax.div(seq, PLANE)
    p = lax.rem(seq, PLANE)
    piece = head_count * DH // PLANE
    model_width = y_count * head_count * DH

    def in_plane(offset):
        return lax.rem(p + offset, PLANE)

    def in_column(offset):
        return lax.rem(z + offset, z_count)

    def seq_of(at_z, at_p):
        return at_z * PLANE + at_p

    hops = sorted({d % z_count for d in NEAR + FAR} | {-d % z_count for d in NEAR + FAR})
    barrier = pltpu.get_barrier_semaphore()
    for k in range(1, PLANE):
        pl.semaphore_signal(barrier, inc=1, device_id=(seq_of(z, in_plane(k)), y), device_id_type=MESH)
    for d in hops:
        pl.semaphore_signal(barrier, inc=1, device_id=(seq_of(in_column(d), p), y), device_id_type=MESH)
    for k in range(1, y_count):
        pl.semaphore_signal(barrier, inc=1, device_id=(seq, lax.rem(y + k, y_count)), device_id_type=MESH)

    def remote(source, target, send, recv, seq_to, y_to):
        return pltpu.make_async_remote_copy(
            src_ref=source, dst_ref=target, send_sem=send, recv_sem=recv,
            device_id=(seq_to, y_to), device_id_type=MESH,
        )

    def plane_out(total, plane, send, recv):
        copies = []
        for k in (4, 3, 5, 2, 6, 1, 7):
            to = in_plane(k)
            copy = remote(total.at[to], plane.at[k], send.at[k], recv.at[k], seq_of(z, to), y)
            copy.start()
            copies.append(copy)
        return copies

    def column_out(source, slots, send, recv, distances, sign):
        copies = []
        for d in reversed(distances):
            to = in_column((sign * d) % z_count)
            at = (NEAR + FAR).index(d)
            copy = remote(
                source, slots.at[distances.index(d)], send.at[at], recv.at[at], seq_of(to, p), y
            )
            copy.start()
            copies.append(copy)
        return copies

    def plane_back(stage, target, send, recv):
        copies = []
        for k in (4, 3, 5, 2, 6, 1, 7):
            to = in_plane(k)
            copy = remote(stage.at[to], target.at[p], send.at[k], recv.at[k], seq_of(z, to), y)
            copy.start()
            copies.append(copy)
        return copies

    def finish(copies):
        for copy in copies:
            copy.wait()

    def plane_sum(total, plane):
        value = total[p]
        for k in range(1, PLANE):
            value = value + plane[k]
        return value

    def reached(d, reverse):
        return (z + d < z_count) if reverse else (z >= d)

    def gated(value, d, reverse):
        state = jnp.where(reached(d, reverse), value[:piece], 0.0)
        if value.shape[0] == piece:
            return state
        return jnp.concatenate([state, value[piece:]], axis=0)

    def stages(carried, total, plane, stage, reverse):
        for target in range(PLANE):
            value = carried
            for k in range(PLANE):
                source = lax.rem(p + PLANE - k, PLANE)
                part = (total[p] if k == 0 else plane[k])[:piece]
                wanted = (source > target) if reverse else (source < target)
                value = value + jnp.where(wanted, part, 0.0)
            stage[target] = value

    row = lax.broadcasted_iota(jnp.int32, (BLOCK, BLOCK), 0)
    col = lax.broadcasted_iota(jnp.int32, (BLOCK, BLOCK), 1)
    causal = row >= col

    def at(ref, b, h):
        return ref[b * BLOCK : (b + 1) * BLOCK, h * DH : (h + 1) * DH]

    def cols(h):
        return slice(h * DH, (h + 1) * DH)

    half = DH // piece

    def put_total(total, h, value):
        for i in range(half):
            total[h * half + i, 0:piece] = value[i * piece : (i + 1) * piece]

    def carried_state(ref, h):
        return jnp.concatenate([ref[h * half + i] for i in range(half)], axis=0)

    for h in range(head_count):
        first = dot(at(k_ref, 0, h), at(v_ref, 0, h), 0, 0)
        second = dot(at(k_ref, 1, h), at(v_ref, 1, h), 0, 0)
        inner[h] = first
        put_total(total_f, h, first + second)

    pl.semaphore_wait(barrier, PLANE - 1 + len(hops) + y_count - 1)
    sent = plane_out(total_f, plane_f, fa_send, fa_recv)

    for h in range(head_count):
        for b in range(block_count):
            products = dot(at(q_ref, b, h), at(k_ref, b, h), 1, 1)
            kept = jnp.where(causal, products, 0.0).astype(BF16)
            scores[b * BLOCK : (b + 1) * BLOCK, cols(h)] = kept
            value = dot(kept, at(v_ref, b, h), 1, 0)
            if b == 1:
                value = value + dot_wide(at(q_ref, b, h), inner[h], 0)
            att[b * BLOCK : (b + 1) * BLOCK, cols(h)] = value

    def scan(total, plane, step, near, window, far, stage, target, sems, sent, reverse):
        b_send, b_recv, c_send, c_recv = sems
        sign = -1 if reverse else 1
        finish(sent)
        step[...] = plane_sum(total, plane)
        sent = column_out(step, near, b_send, b_recv, NEAR, sign)
        finish(sent)
        before = gated(near[0], NEAR[0], reverse)
        for i in range(1, len(NEAR)):
            before = before + gated(near[i], NEAR[i], reverse)
        window[...] = before + step[...]
        sent = column_out(window, far, b_send, b_recv, FAR, sign)
        finish(sent)
        carried = before[:piece]
        for i in range(len(FAR)):
            carried = carried + gated(far[i], FAR[i], reverse)[:piece]
        stages(carried, total, plane, stage, reverse)
        sent = plane_back(stage, target, c_send, c_recv)
        target[p] = stage[p]
        return sent

    sent = scan(
        total_f, plane_f, step_f, near_f, window_f, far_f, stage_f, earlier,
        (fb_send, fb_recv, fc_send, fc_recv), sent, False,
    )
    finish(sent)

    squares = jnp.zeros((block_count * BLOCK, DH), F32)
    weighted = jnp.zeros((block_count * BLOCK, DH), F32)
    for h in range(head_count):
        value = att[:, cols(h)] + dot_wide(q_ref[:, cols(h)], carried_state(earlier, h), 0)
        att[:, cols(h)] = value
        squares = squares + value * value
        weighted = weighted + gain_ref[:, cols(h)] * g_ref[:, cols(h)].astype(F32) * value
    tokens = block_count * BLOCK
    square_row = jnp.sum(squares.T, axis=0, keepdims=True)
    weighted_row = jnp.sum(weighted.T, axis=0, keepdims=True)
    line = lax.broadcasted_iota(jnp.int32, (8, tokens), 0)
    sums[0] = jnp.where(line == 0, square_row, jnp.where(line == 1, weighted_row, 0.0))
    sent = []
    for k in (4, 3, 5, 2, 6, 1, 7):
        copy = remote(sums.at[0], sums.at[k], h_send.at[k], h_recv.at[k], seq, lax.rem(y + k, y_count))
        copy.start()
        sent.append(copy)
    finish(sent)
    whole = sums[0]
    for k in range(1, y_count):
        whole = whole + sums[k]
    inverse_row = 1.0 / jnp.sqrt(whole[0:1] / model_width + EPSILON)
    pull_row = inverse_row * inverse_row * inverse_row * whole[1:2] / model_width
    inverse = jnp.broadcast_to(inverse_row, (DH, tokens)).T
    pull = jnp.broadcast_to(pull_row, (DH, tokens)).T

    gain_line = lax.broadcasted_iota(jnp.int32, (8, DH), 0)
    gain_part = jnp.zeros((8, DH), F32)
    for h in range(head_count):
        value = att[:, cols(h)]
        scaled = g_ref[:, cols(h)].astype(F32) * inverse
        gain_sum = jnp.sum(scaled * value, axis=0, keepdims=True)
        gain_part = jnp.where(gain_line == h, gain_sum, gain_part)
        grad = (gain_ref[:, cols(h)] * scaled - value * pull).astype(BF16)
        grad_att[:, cols(h)] = grad
        first = dot(at(q_ref, 0, h), grad[:BLOCK], 0, 0)
        second = dot(at(q_ref, 1, h), grad[BLOCK:], 0, 0)
        inner_b = second
        att[0:DH, cols(h)] = inner_b
        put_total(total_b, h, first + second)
    for s in range(PLANE):
        total_b[s, piece : piece + 8] = gain_part
    sent = plane_out(total_b, plane_b, ba_send, ba_recv)

    for h in range(head_count):
        state = carried_state(earlier, h)
        after_first = att[0:DH, cols(h)]
        for b in range(block_count):
            rows = slice(b * BLOCK, (b + 1) * BLOCK)
            grad = grad_att[rows, cols(h)]
            products = dot(grad, at(v_ref, b, h), 1, 1)
            grad_scores = jnp.where(causal, products, 0.0).astype(BF16)
            here = state + inner[h] if b == 1 else state
            value = dot(grad_scores, at(k_ref, b, h), 1, 0) + dot_wide(grad, here, 1)
            gq_ref[rows, cols(h)] = value.astype(BF16)
            key = dot(grad_scores, at(q_ref, b, h), 0, 0)
            val = dot(scores[rows, cols(h)], grad, 0, 0)
            if b == 0:
                key = key + dot_wide(at(v_ref, b, h), after_first, 1)
                val = val + dot_wide(at(k_ref, b, h), after_first, 0)
            gk_part[rows, cols(h)] = key
            gv_part[rows, cols(h)] = val

    sent = scan(
        total_b, plane_b, step_b, near_b, window_b, far_b, stage_b, later,
        (bb_send, bb_recv, bc_send, bc_recv), sent, True,
    )
    gg_ref[...] = window_b[piece : piece + 8] + far_b[0, piece : piece + 8] + far_b[1, piece : piece + 8]
    finish(sent)
    for h in range(head_count):
        after = carried_state(later, h)
        key = gk_part[:, cols(h)] + dot_wide(v_ref[:, cols(h)], after, 1)
        gk_ref[:, cols(h)] = key.astype(BF16)
        val = gv_part[:, cols(h)] + dot_wide(k_ref[:, cols(h)], after, 0)
        gv_ref[:, cols(h)] = val.astype(BF16)


def local(z_count, queries, key_vectors, value_vectors, out_grad, norm_gain):
    tokens, features = queries.shape
    head_count = features // DH
    block_count = tokens // BLOCK
    y_count = lax.axis_size("head")
    piece = head_count * DH // PLANE
    like = jax.ShapeDtypeStruct((tokens, features), BF16)
    vmem = pl.BlockSpec(memory_space=pltpu.VMEM)

    def scan_scratch(rows):
        return [
            pltpu.VMEM((PLANE, rows, DH), F32),
            pltpu.VMEM((PLANE, rows, DH), F32),
            pltpu.VMEM((rows, DH), F32),
            pltpu.VMEM((len(NEAR), rows, DH), F32),
            pltpu.VMEM((rows, DH), F32),
            pltpu.VMEM((len(FAR), rows, DH), F32),
            pltpu.VMEM((PLANE, piece, DH), F32),
        ]

    far_count = len(NEAR) + len(FAR)
    scan_sems = [pltpu.SemaphoreType.DMA((n,)) for n in (PLANE, PLANE, far_count, far_count, PLANE, PLANE)]
    outs = pl.pallas_call(
        functools.partial(kernel, z_count, y_count, head_count, block_count),
        out_shape=(like, like, like, jax.ShapeDtypeStruct((8, DH), F32)),
        in_specs=[vmem] * 5,
        out_specs=(vmem,) * 4,
        scratch_shapes=[
            pltpu.VMEM((head_count, DH, DH), F32),
            pltpu.VMEM((tokens, features), F32),
            pltpu.VMEM((tokens, features), BF16),
            pltpu.VMEM((tokens, features), BF16),
            pltpu.VMEM((tokens, features), F32),
            pltpu.VMEM((tokens, features), F32),
            pltpu.VMEM((PLANE, piece, DH), F32),
            pltpu.VMEM((PLANE, piece, DH), F32),
            *scan_scratch(piece),
            *scan_scratch(piece + 8),
            pltpu.VMEM((y_count, 8, tokens), F32),
            *scan_sems,
            *scan_sems,
            pltpu.SemaphoreType.DMA((y_count,)),
            pltpu.SemaphoreType.DMA((y_count,)),
        ],
        compiler_params=pltpu.CompilerParams(
            collective_id=0, has_side_effects=True, vmem_limit_bytes=48 * 1024 * 1024
        ),
        name="linear_attention_backward",
    )(queries, key_vectors, value_vectors, out_grad, norm_gain.reshape(1, features))
    return outs[0], outs[1], outs[2], outs[3][:head_count].reshape(features)


def solution(mesh):
    in_specs = (P("seq", "head"), P("seq", "head"), P("seq", "head"), P("seq", "head"), P("head"))
    out_specs = (P("seq", "head"), P("seq", "head"), P("seq", "head"), P("head"))
    body = functools.partial(local, mesh.shape["seq"] // PLANE)
    return jax.shard_map(body, mesh=mesh, in_specs=in_specs, out_specs=out_specs, check_vma=False)
```

```python
import functools

import jax
import jax.numpy as jnp
from jax import lax
from jax.experimental import pallas as pl
from jax.experimental.pallas import tpu as pltpu
from jax.sharding import PartitionSpec as P

DH = 128
BLOCK = 128
PLANE = 8
NEAR = (2, -2, 1, -1)
FAR = ((4, (-2, -1, 0, 1)), (-4, (-1, 0, 1)))
EPSILON = 1e-06
CHUNKS = 2
MESH = pl.DeviceIdType.MESH
F32 = jnp.float32
BF16 = jnp.bfloat16


def dot(left, right, left_dim, right_dim):
    return lax.dot_general(
        left, right, (((left_dim,), (right_dim,)), ((), ())), preferred_element_type=F32
    )


def split(wide):
    high = wide.astype(BF16)
    low = (wide - high.astype(F32)).astype(BF16)
    return high, low


def dot_wide(left, wide, wide_dim):
    high, low = split(wide)
    return dot(left, high, 1, wide_dim) + dot(left, low, 1, wide_dim)


def kernel(
    z_count, y_count, head_count, block_count,
    q_hbm, k_hbm, v_hbm, g_hbm, gain_hbm,
    gq_ref, gk_ref, gv_ref, gg_ref,
    q_ref, k_ref, v_ref, g_ref, gain_ref,
    inner, inner_b, att, scores, grad_att, gk_part, gv_part, earlier, later,
    total_f, plane_f, step_f, near_f, window_f, far_f, stage_f,
    total_b, plane_b, step_b, near_b, window_b, far_b, stage_b,
    sums,
    fa_send, fa_recv, fb_send, fb_recv, fc_send, fc_recv,
    ba_send, ba_recv, bb_send, bb_recv, bc_send, bc_recv,
    h_send, h_recv, load_sem,
):
    loads = {}
    pairs = ((k_hbm, k_ref), (v_hbm, v_ref), (q_hbm, q_ref), (g_hbm, g_ref), (gain_hbm, gain_ref))
    for i, (source, target) in enumerate(pairs):
        loads[i] = pltpu.make_async_copy(source, target, load_sem.at[i])
        if i < 2:
            loads[i].start()

    seq = lax.axis_index("seq")
    y = lax.axis_index("head")
    z = lax.div(seq, PLANE)
    p = lax.rem(seq, PLANE)
    heads_each = head_count // CHUNKS
    piece = heads_each * DH // PLANE
    model_width = y_count * head_count * DH

    def in_plane(offset):
        return lax.rem(p + offset, PLANE)

    def in_column(offset):
        return lax.rem(z + offset, z_count)

    def seq_of(at_z, at_p):
        return at_z * PLANE + at_p

    hops = NEAR + tuple(d for d, _ in FAR)
    barrier = pltpu.get_barrier_semaphore()
    for k in range(1, PLANE):
        pl.semaphore_signal(barrier, inc=1, device_id=(seq_of(z, in_plane(k)), y), device_id_type=MESH)
    for d in hops:
        pl.semaphore_signal(barrier, inc=1, device_id=(seq_of(in_column(d % z_count), p), y), device_id_type=MESH)
    for k in range(1, y_count):
        pl.semaphore_signal(barrier, inc=1, device_id=(seq, lax.rem(y + k, y_count)), device_id_type=MESH)

    for i in range(2, len(pairs)):
        loads[i].start()
    unsent = []

    def remote(source, target, send, recv, seq_to, y_to):
        copy = pltpu.make_async_remote_copy(
            src_ref=source, dst_ref=target, send_sem=send, recv_sem=recv,
            device_id=(seq_to, y_to), device_id_type=MESH,
        )
        copy.start()
        unsent.append(copy)
        return copy

    def arrived(copies):
        for copy in copies:
            copy.wait_recv()

    row = lax.broadcasted_iota(jnp.int32, (BLOCK, BLOCK), 0)
    col = lax.broadcasted_iota(jnp.int32, (BLOCK, BLOCK), 1)
    causal = row >= col
    part_rows = DH // PLANE * heads_each
    halves = DH // part_rows if part_rows < DH else 1

    def at(ref, b, h):
        return ref[b * BLOCK : (b + 1) * BLOCK, h * DH : (h + 1) * DH]

    def cols(h):
        return slice(h * DH, (h + 1) * DH)

    def put_total(total, h, value):
        c, place = divmod(h, heads_each)
        for i in range(halves):
            total[c, place * halves + i, 0:piece] = value[i * piece : (i + 1) * piece]

    def carried_state(ref, h):
        c, place = divmod(h, heads_each)
        return jnp.concatenate([ref[c, place * halves + i] for i in range(halves)], axis=0)

    class Scan:
        def __init__(self, refs, target, sems, reverse):
            self.total, self.plane, self.step, self.near, self.window, self.far, self.stage = refs
            self.target = target
            self.a_send, self.a_recv, self.b_send, self.b_recv, self.c_send, self.c_recv = sems
            self.reverse = reverse
            self.flying = {}
            self.before = {}

        def rows(self, c):
            return piece + 8 if self.reverse and c == CHUNKS - 1 else piece

        def around(self, c, place, n):
            if place == 0:
                return self.step[c, 0:n]
            return self.near[c, NEAR.index(-place), 0:n]

        def collect(self, c, distance, places):
            n = self.rows(c)
            here = z_count - 1 - z if self.reverse else z
            target = lax.rem(here + distance % z_count, z_count)
            state = None
            for place in places:
                behind = (distance - place) % z_count
                value = self.around(c, place, n)
                kept = jnp.where(target >= behind, value[:piece], 0.0)
                state = kept if state is None else state + kept
            if n == piece:
                return state
            gain = self.around(c, places[0], n)[piece:]
            for place in places[1:]:
                gain = gain + self.around(c, place, n)[piece:]
            return jnp.concatenate([state, gain], axis=0)

        def plane_out(self, c):
            n = self.rows(c)
            self.flying[c] = []
            for k in (4, 3, 5, 2, 6, 1, 7):
                to = in_plane(k)
                self.flying[c].append(remote(
                    self.total.at[c, to, 0:n], self.plane.at[c, p, 0:n],
                    self.a_send.at[c, k], self.a_recv.at[c, k], seq_of(z, to), y,
                ))
            self.plane[c, p] = self.total[c, p]

        def column_out(self, c, i, distance, source, target):
            to = in_column((-distance if self.reverse else distance) % z_count)
            return remote(source, target, self.b_send.at[c, i], self.b_recv.at[c, i], seq_of(to, p), y)

        def near_out(self, c):
            n = self.rows(c)
            arrived(self.flying[c])
            value = self.plane[c, 0, 0:n]
            for s in range(1, PLANE):
                value = value + self.plane[c, s, 0:n]
            self.step[c, 0:n] = value
            self.flying[c] = [
                self.column_out(c, i, d, self.step.at[c, 0:n], self.near.at[c, i, 0:n])
                for i, d in enumerate(NEAR)
            ]

        def far_out(self, c):
            n = self.rows(c)
            arrived(self.flying[c])
            self.flying[c] = []
            for i, (d, places) in enumerate(FAR):
                self.window[c, i, 0:n] = self.collect(c, d, places)
                self.flying[c].append(self.column_out(
                    c, len(NEAR) + i, d, self.window.at[c, i, 0:n], self.far.at[c, i, 0:n]
                ))
            self.before[c] = self.collect(c, 0, tuple(-d for d in NEAR))

        def plane_back(self, c):
            arrived(self.flying[c])
            value = self.before[c][:piece]
            for i in range(len(FAR)):
                value = value + self.far[c, i, 0:piece]
            order = range(PLANE - 1, -1, -1) if self.reverse else range(PLANE)
            for s in order:
                self.stage[c, s] = value
                value = value + self.plane[c, s, 0:piece]
            self.flying[c] = []
            for k in (4, 3, 5, 2, 6, 1, 7):
                to = in_plane(k)
                self.flying[c].append(remote(
                    self.stage.at[c, to], self.target.at[c, p],
                    self.c_send.at[c, k], self.c_recv.at[c, k], seq_of(z, to), y,
                ))
            self.target[c, p] = self.stage[c, p]

        def landed(self, c):
            arrived(self.flying[c])

    forward = Scan(
        (total_f, plane_f, step_f, near_f, window_f, far_f, stage_f), earlier,
        (fa_send, fa_recv, fb_send, fb_recv, fc_send, fc_recv), False,
    )
    backward = Scan(
        (total_b, plane_b, step_b, near_b, window_b, far_b, stage_b), later,
        (ba_send, ba_recv, bb_send, bb_recv, bc_send, bc_recv), True,
    )

    def of_chunk(c):
        return range(c * heads_each, (c + 1) * heads_each)

    loads[0].wait()
    loads[1].wait()
    for c in range(CHUNKS):
        for h in of_chunk(c):
            first = dot(at(k_ref, 0, h), at(v_ref, 0, h), 0, 0)
            second = dot(at(k_ref, 1, h), at(v_ref, 1, h), 0, 0)
            inner[h] = first
            put_total(total_f, h, first + second)
        if c == 0:
            pl.semaphore_wait(barrier, PLANE - 1 + len(hops) + y_count - 1)
        forward.plane_out(c)

    def inside(h):
        for b in range(block_count):
            products = dot(at(q_ref, b, h), at(k_ref, b, h), 1, 1)
            kept = jnp.where(causal, products, 0.0).astype(BF16)
            scores[b * BLOCK : (b + 1) * BLOCK, cols(h)] = kept
            value = dot(kept, at(v_ref, b, h), 1, 0)
            if b == 1:
                value = value + dot_wide(at(q_ref, b, h), inner[h], 0)
            att[b * BLOCK : (b + 1) * BLOCK, cols(h)] = value

    loads[2].wait()
    for h in range(head_count // 2):
        inside(h)
    for c in range(CHUNKS):
        forward.near_out(c)
    for h in range(head_count // 2, head_count):
        inside(h)
    for c in range(CHUNKS):
        forward.far_out(c)
    for c in range(CHUNKS):
        forward.plane_back(c)
    loads[3].wait()
    loads[4].wait()

    tokens = block_count * BLOCK
    squares = jnp.zeros((tokens, DH), F32)
    weighted = jnp.zeros((tokens, DH), F32)
    for c in range(CHUNKS):
        forward.landed(c)
        for h in of_chunk(c):
            value = att[:, cols(h)] + dot_wide(q_ref[:, cols(h)], carried_state(earlier, h), 0)
            att[:, cols(h)] = value
            squares = squares + value * value
            weighted = weighted + gain_ref[:, cols(h)] * g_ref[:, cols(h)].astype(F32) * value
    square_row = jnp.sum(squares.T, axis=0, keepdims=True)
    weighted_row = jnp.sum(weighted.T, axis=0, keepdims=True)
    line = lax.broadcasted_iota(jnp.int32, (8, tokens), 0)
    sums[0] = jnp.where(line == 0, square_row, jnp.where(line == 1, weighted_row, 0.0))
    sent = []
    for k in (4, 3, 5, 2, 6, 1, 7):
        to = lax.rem(y + k, y_count)
        sent.append(remote(sums.at[0], sums.at[k], h_send.at[k], h_recv.at[k], seq, to))
    arrived(sent)
    whole = sums[0]
    for k in range(1, y_count):
        whole = whole + sums[k]
    inverse_row = 1.0 / jnp.sqrt(whole[0:1] / model_width + EPSILON)
    pull_row = inverse_row * inverse_row * inverse_row * whole[1:2] / model_width
    inverse = jnp.broadcast_to(inverse_row, (DH, tokens)).T
    pull = jnp.broadcast_to(pull_row, (DH, tokens)).T

    gain_line = lax.broadcasted_iota(jnp.int32, (8, DH), 0)
    gain_part = jnp.zeros((8, DH), F32)
    for c in range(CHUNKS):
        for h in of_chunk(c):
            value = att[:, cols(h)]
            scaled = g_ref[:, cols(h)].astype(F32) * inverse
            gain_sum = jnp.sum(scaled * value, axis=0, keepdims=True)
            gain_part = jnp.where(gain_line == h, gain_sum, gain_part)
            grad = (gain_ref[:, cols(h)] * scaled - value * pull).astype(BF16)
            grad_att[:, cols(h)] = grad
            first = dot(at(q_ref, 0, h), grad[:BLOCK], 0, 0)
            second = dot(at(q_ref, 1, h), grad[BLOCK:], 0, 0)
            inner_b[h] = second
            put_total(total_b, h, first + second)
        if c == CHUNKS - 1:
            for s in range(PLANE):
                total_b[c, s, piece : piece + 8] = gain_part
        backward.plane_out(c)

    def inside_grads(h):
        state = carried_state(earlier, h)
        for b in range(block_count):
            rows = slice(b * BLOCK, (b + 1) * BLOCK)
            grad = grad_att[rows, cols(h)]
            products = dot(grad, at(v_ref, b, h), 1, 1)
            grad_scores = jnp.where(causal, products, 0.0).astype(BF16)
            here = state + inner[h] if b == 1 else state
            value = dot(grad_scores, at(k_ref, b, h), 1, 0) + dot_wide(grad, here, 1)
            gq_ref[rows, cols(h)] = value.astype(BF16)
            key = dot(grad_scores, at(q_ref, b, h), 0, 0)
            val = dot(scores[rows, cols(h)], grad, 0, 0)
            if b == 0:
                key = key + dot_wide(at(v_ref, b, h), inner_b[h], 1)
                val = val + dot_wide(at(k_ref, b, h), inner_b[h], 0)
            gk_part[rows, cols(h)] = key
            gv_part[rows, cols(h)] = val

    for h in range(head_count // 2):
        inside_grads(h)
    for c in range(CHUNKS):
        backward.near_out(c)
    for h in range(head_count // 2, 3 * head_count // 4):
        inside_grads(h)
    for c in range(CHUNKS):
        backward.far_out(c)
    for h in range(3 * head_count // 4, head_count):
        inside_grads(h)
    for c in range(CHUNKS):
        backward.plane_back(c)
    last = CHUNKS - 1
    gain_rows = slice(piece, piece + 8)
    whole_gain = backward.before[last][gain_rows] + step_b[last, gain_rows]
    for i in range(len(FAR)):
        whole_gain = whole_gain + far_b[last, i, gain_rows]
    for h in range(head_count):
        gg_ref[:, cols(h)] = whole_gain[h : h + 1]
    for c in range(CHUNKS):
        backward.landed(c)
        for h in of_chunk(c):
            after = carried_state(later, h)
            key = gk_part[:, cols(h)] + dot_wide(v_ref[:, cols(h)], after, 1)
            gk_ref[:, cols(h)] = key.astype(BF16)
            val = gv_part[:, cols(h)] + dot_wide(k_ref[:, cols(h)], after, 0)
            gv_ref[:, cols(h)] = val.astype(BF16)
    for copy in unsent:
        copy.wait_send()


def write_out(a_ref, b_ref, c_ref, d_ref, a_hbm, b_hbm, c_hbm, d_hbm, sem):
    copies = []
    pairs = ((a_ref, a_hbm), (b_ref, b_hbm), (c_ref, c_hbm), (d_ref, d_hbm))
    for i, (source, target) in enumerate(pairs):
        copies.append(pltpu.make_async_copy(source, target, sem.at[i]))
        copies[-1].start()
    for copy in copies:
        copy.wait()


def local(z_count, queries, key_vectors, value_vectors, out_grad, norm_gain):
    tokens, features = queries.shape
    head_count = features // DH
    block_count = tokens // BLOCK
    y_count = lax.axis_size("head")
    piece = head_count // CHUNKS * DH // PLANE
    like = jax.ShapeDtypeStruct((tokens, features), BF16)
    shapes = (like, like, like, jax.ShapeDtypeStruct((1, features), F32))
    vmem = pl.BlockSpec(memory_space=pltpu.VMEM)
    hbm = pl.BlockSpec(memory_space=pltpu.HBM)

    def scan_scratch(rows):
        return [
            pltpu.VMEM((CHUNKS, PLANE, rows, DH), F32),
            pltpu.VMEM((CHUNKS, PLANE, rows, DH), F32),
            pltpu.VMEM((CHUNKS, rows, DH), F32),
            pltpu.VMEM((CHUNKS, len(NEAR), rows, DH), F32),
            pltpu.VMEM((CHUNKS, len(FAR), rows, DH), F32),
            pltpu.VMEM((CHUNKS, len(FAR), rows, DH), F32),
            pltpu.VMEM((CHUNKS, PLANE, piece, DH), F32),
        ]

    z_copies = len(NEAR) + len(FAR)
    scan_sems = [
        pltpu.SemaphoreType.DMA((CHUNKS, n)) for n in (PLANE, PLANE, z_copies, z_copies, PLANE, PLANE)
    ]
    operands = (queries, key_vectors, value_vectors, out_grad, norm_gain.reshape(1, features))
    results = pl.pallas_call(
        functools.partial(kernel, z_count, y_count, head_count, block_count),
        out_shape=shapes,
        in_specs=[hbm] * 5,
        out_specs=(vmem,) * 4,
        scratch_shapes=[
            *[pltpu.VMEM((tokens, features), BF16)] * 4,
            pltpu.VMEM((1, features), F32),
            pltpu.VMEM((head_count, DH, DH), F32),
            pltpu.VMEM((head_count, DH, DH), F32),
            pltpu.VMEM((tokens, features), F32),
            pltpu.VMEM((tokens, features), BF16),
            pltpu.VMEM((tokens, features), BF16),
            pltpu.VMEM((tokens, features), F32),
            pltpu.VMEM((tokens, features), F32),
            pltpu.VMEM((CHUNKS, PLANE, piece, DH), F32),
            pltpu.VMEM((CHUNKS, PLANE, piece, DH), F32),
            *scan_scratch(piece),
            *scan_scratch(piece + 8),
            pltpu.VMEM((y_count, 8, tokens), F32),
            *scan_sems,
            *scan_sems,
            pltpu.SemaphoreType.DMA((y_count,)),
            pltpu.SemaphoreType.DMA((y_count,)),
            pltpu.SemaphoreType.DMA((5,)),
        ],
        compiler_params=pltpu.CompilerParams(
            collective_id=0, has_side_effects=True, vmem_limit_bytes=32 * 1024 * 1024
        ),
        name="linear_attention_backward",
    )(*[pltpu.with_memory_space_constraint(x, pltpu.HBM) for x in operands])
    outs = pl.pallas_call(
        write_out,
        out_shape=shapes,
        in_specs=[vmem] * 4,
        out_specs=(hbm,) * 4,
        scratch_shapes=[pltpu.SemaphoreType.DMA((4,))],
        name="write_out",
    )(*[pltpu.with_memory_space_constraint(x, pltpu.VMEM) for x in results])
    return outs[0], outs[1], outs[2], outs[3].reshape(features)


def solution(mesh):
    in_specs = (P("seq", "head"), P("seq", "head"), P("seq", "head"), P("seq", "head"), P("head"))
    out_specs = (P("seq", "head"), P("seq", "head"), P("seq", "head"), P("head"))
    body = functools.partial(local, mesh.shape["seq"] // PLANE)
    return jax.shard_map(body, mesh=mesh, in_specs=in_specs, out_specs=out_specs, check_vma=False)
```

```python
import functools

import jax
import jax.numpy as jnp
from jax import lax
from jax.experimental import pallas as pl
from jax.experimental.pallas import tpu as pltpu
from jax.sharding import PartitionSpec as P

DH = 128
BLOCK = 128
PLANE = 8
NEAR = (2, -2, 1, -1)
FAR = ((4, (-2, -1, 0, 1)), (-4, (-1, 0, 1)))
EPSILON = 1e-06
CHUNKS = 2
MESH = pl.DeviceIdType.MESH
F32 = jnp.float32
BF16 = jnp.bfloat16


def dot(left, right, left_dim, right_dim):
    return lax.dot_general(
        left, right, (((left_dim,), (right_dim,)), ((), ())), preferred_element_type=F32
    )


def split(wide):
    high = wide.astype(BF16)
    low = (wide - high.astype(F32)).astype(BF16)
    return high, low


def dot_wide(left, wide, wide_dim):
    high, low = split(wide)
    return dot(left, high, 1, wide_dim) + dot(left, low, 1, wide_dim)


def kernel(
    z_count, y_count, head_count, block_count,
    q_hbm, k_hbm, v_hbm, g_hbm, gain_hbm,
    gq_ref, gk_ref, gv_ref, gg_ref,
    q_ref, k_ref, v_ref, g_ref, gain_ref,
    inner, inner_b, att, scores, grad_att, gk_part, gv_part, earlier, later,
    total_f, plane_f, step_f, near_f, window_f, far_f, stage_f,
    total_b, plane_b, step_b, near_b, window_b, far_b, stage_b,
    sums,
    f_send, f_recv, b_send, b_recv, h_send, h_recv, load_sem,
):
    loads = {}
    pairs = ((k_hbm, k_ref), (v_hbm, v_ref), (q_hbm, q_ref), (g_hbm, g_ref), (gain_hbm, gain_ref))
    for i, (source, target) in enumerate(pairs):
        loads[i] = pltpu.make_async_copy(source, target, load_sem.at[i])
        if i < 2:
            loads[i].start()

    seq = lax.axis_index("seq")
    y = lax.axis_index("head")
    z = lax.div(seq, PLANE)
    p = lax.rem(seq, PLANE)
    heads_each = head_count // CHUNKS
    piece = heads_each * DH // PLANE
    model_width = y_count * head_count * DH

    def in_plane(offset):
        return lax.rem(p + offset, PLANE)

    def in_column(offset):
        return lax.rem(z + offset, z_count)

    def seq_of(at_z, at_p):
        return at_z * PLANE + at_p

    hops = NEAR + tuple(d for d, _ in FAR)
    barrier = pltpu.get_barrier_semaphore()
    for k in range(1, PLANE):
        pl.semaphore_signal(barrier, inc=1, device_id=(seq_of(z, in_plane(k)), y), device_id_type=MESH)
    for d in hops:
        pl.semaphore_signal(barrier, inc=1, device_id=(seq_of(in_column(d % z_count), p), y), device_id_type=MESH)
    for k in range(1, y_count):
        pl.semaphore_signal(barrier, inc=1, device_id=(seq, lax.rem(y + k, y_count)), device_id_type=MESH)

    for i in range(2, len(pairs)):
        loads[i].start()
    unsent = []

    def remote(source, target, send, recv, seq_to, y_to):
        copy = pltpu.make_async_remote_copy(
            src_ref=source, dst_ref=target, send_sem=send, recv_sem=recv,
            device_id=(seq_to, y_to), device_id_type=MESH,
        )
        copy.start()

    def bytes_of(ref, sem):
        pltpu.make_async_copy(ref, ref, sem).wait()

    def flying(ref, send, recv):
        unsent.append((ref, send))
        return ref, recv

    row = lax.broadcasted_iota(jnp.int32, (BLOCK, BLOCK), 0)
    col = lax.broadcasted_iota(jnp.int32, (BLOCK, BLOCK), 1)
    causal = row >= col
    part_rows = DH // PLANE * heads_each
    halves = DH // part_rows if part_rows < DH else 1

    def at(ref, b, h):
        return ref[b * BLOCK : (b + 1) * BLOCK, h * DH : (h + 1) * DH]

    def cols(h):
        return slice(h * DH, (h + 1) * DH)

    def put_total(total, h, value):
        c, place = divmod(h, heads_each)
        for i in range(halves):
            total[c, place * halves + i, 0:piece] = value[i * piece : (i + 1) * piece]

    def carried_state(ref, h):
        c, place = divmod(h, heads_each)
        return jnp.concatenate([ref[c, place * halves + i] for i in range(halves)], axis=0)

    class Scan:
        def __init__(self, refs, target, sems, reverse):
            self.total, self.plane, self.step, self.near, self.window, self.far, self.stage = refs
            self.target = target
            self.send, self.recv = sems
            self.reverse = reverse
            self.flying = {}
            self.before = {}

        def fly(self, c, phase, ref):
            self.flying[c] = flying(ref, self.send.at[c, phase], self.recv.at[c, phase])

        def rows(self, c):
            return piece + 8 if self.reverse and c == CHUNKS - 1 else piece

        def around(self, c, place, n):
            if place == 0:
                return self.step[c, 0:n]
            return self.near[c, NEAR.index(-place), 0:n]

        def collect(self, c, distance, places):
            n = self.rows(c)
            here = z_count - 1 - z if self.reverse else z
            target = lax.rem(here + distance % z_count, z_count)
            state = None
            for place in places:
                behind = (distance - place) % z_count
                value = self.around(c, place, n)
                kept = jnp.where(target >= behind, value[:piece], 0.0)
                state = kept if state is None else state + kept
            if n == piece:
                return state
            gain = self.around(c, places[0], n)[piece:]
            for place in places[1:]:
                gain = gain + self.around(c, place, n)[piece:]
            return jnp.concatenate([state, gain], axis=0)

        def plane_out(self, c):
            n = self.rows(c)
            for k in (4, 3, 5, 2, 6, 1, 7):
                to = in_plane(k)
                remote(
                    self.total.at[c, to, 0:n], self.plane.at[c, p, 0:n],
                    self.send.at[c, 0], self.recv.at[c, 0], seq_of(z, to), y,
                )
            self.fly(c, 0, self.plane.at[c, 0 : PLANE - 1, 0:n])
            self.plane[c, p] = self.total[c, p]

        def column_out(self, c, phase, distance, source, target):
            to = in_column((-distance if self.reverse else distance) % z_count)
            remote(source, target, self.send.at[c, phase], self.recv.at[c, phase], seq_of(to, p), y)

        def near_out(self, c):
            n = self.rows(c)
            bytes_of(*self.flying[c])
            value = self.plane[c, 0, 0:n]
            for s in range(1, PLANE):
                value = value + self.plane[c, s, 0:n]
            self.step[c, 0:n] = value
            for i, d in enumerate(NEAR):
                self.column_out(c, 1, d, self.step.at[c, 0:n], self.near.at[c, i, 0:n])
            self.fly(c, 1, self.near.at[c, :, 0:n])

        def far_out(self, c):
            n = self.rows(c)
            bytes_of(*self.flying[c])
            for i, (d, places) in enumerate(FAR):
                self.window[c, i, 0:n] = self.collect(c, d, places)
                self.column_out(c, 2, d, self.window.at[c, i, 0:n], self.far.at[c, i, 0:n])
            self.fly(c, 2, self.far.at[c, :, 0:n])
            self.before[c] = self.collect(c, 0, tuple(-d for d in NEAR))

        def plane_back(self, c):
            bytes_of(*self.flying[c])
            value = self.before[c][:piece]
            for i in range(len(FAR)):
                value = value + self.far[c, i, 0:piece]
            order = range(PLANE - 1, -1, -1) if self.reverse else range(PLANE)
            for s in order:
                self.stage[c, s] = value
                value = value + self.plane[c, s, 0:piece]
            for k in (4, 3, 5, 2, 6, 1, 7):
                to = in_plane(k)
                remote(
                    self.stage.at[c, to], self.target.at[c, p],
                    self.send.at[c, 3], self.recv.at[c, 3], seq_of(z, to), y,
                )
            self.fly(c, 3, self.target.at[c, 0 : PLANE - 1])
            self.target[c, p] = self.stage[c, p]

        def landed(self, c):
            bytes_of(*self.flying[c])

    forward = Scan(
        (total_f, plane_f, step_f, near_f, window_f, far_f, stage_f), earlier,
        (f_send, f_recv), False,
    )
    backward = Scan(
        (total_b, plane_b, step_b, near_b, window_b, far_b, stage_b), later,
        (b_send, b_recv), True,
    )

    def of_chunk(c):
        return range(c * heads_each, (c + 1) * heads_each)

    loads[0].wait()
    loads[1].wait()
    for c in range(CHUNKS):
        for h in of_chunk(c):
            first = dot(at(k_ref, 0, h), at(v_ref, 0, h), 0, 0)
            second = dot(at(k_ref, 1, h), at(v_ref, 1, h), 0, 0)
            inner[h] = first
            put_total(total_f, h, first + second)
        if c == 0:
            pl.semaphore_wait(barrier, PLANE - 1 + len(hops) + y_count - 1)
        forward.plane_out(c)

    def inside(h):
        for b in range(block_count):
            products = dot(at(q_ref, b, h), at(k_ref, b, h), 1, 1)
            kept = jnp.where(causal, products, 0.0).astype(BF16)
            scores[b * BLOCK : (b + 1) * BLOCK, cols(h)] = kept
            value = dot(kept, at(v_ref, b, h), 1, 0)
            if b == 1:
                value = value + dot_wide(at(q_ref, b, h), inner[h], 0)
            att[b * BLOCK : (b + 1) * BLOCK, cols(h)] = value

    loads[2].wait()
    for h in range(head_count // 2):
        inside(h)
    for c in range(CHUNKS):
        forward.near_out(c)
    for h in range(head_count // 2, head_count):
        inside(h)
    for c in range(CHUNKS):
        forward.far_out(c)
    for c in range(CHUNKS):
        forward.plane_back(c)
    loads[3].wait()
    loads[4].wait()

    tokens = block_count * BLOCK
    squares = jnp.zeros((tokens, DH), F32)
    weighted = jnp.zeros((tokens, DH), F32)
    for c in range(CHUNKS):
        forward.landed(c)
        for h in of_chunk(c):
            value = att[:, cols(h)] + dot_wide(q_ref[:, cols(h)], carried_state(earlier, h), 0)
            att[:, cols(h)] = value
            squares = squares + value * value
            weighted = weighted + gain_ref[:, cols(h)] * g_ref[:, cols(h)].astype(F32) * value
    square_row = jnp.sum(squares.T, axis=0, keepdims=True)
    weighted_row = jnp.sum(weighted.T, axis=0, keepdims=True)
    sums[0, 0:1] = square_row
    sums[0, 1:2] = weighted_row
    for k in (4, 3, 5, 2, 6, 1, 7):
        remote(sums.at[0], sums.at[k], h_send, h_recv, seq, lax.rem(y + k, y_count))
    bytes_of(*flying(sums.at[1:y_count], h_send, h_recv))
    whole = sums[0]
    for k in range(1, y_count):
        whole = whole + sums[k]
    inverse_row = 1.0 / jnp.sqrt(whole[0:1] / model_width + EPSILON)
    pull_row = inverse_row * inverse_row * inverse_row * whole[1:2] / model_width
    inverse = jnp.broadcast_to(inverse_row, (DH, tokens)).T
    pull = jnp.broadcast_to(pull_row, (DH, tokens)).T

    gain_line = lax.broadcasted_iota(jnp.int32, (8, DH), 0)
    gain_part = jnp.zeros((8, DH), F32)
    for c in range(CHUNKS):
        for h in of_chunk(c):
            value = att[:, cols(h)]
            scaled = g_ref[:, cols(h)].astype(F32) * inverse
            gain_sum = jnp.sum(scaled * value, axis=0, keepdims=True)
            gain_part = jnp.where(gain_line == h, gain_sum, gain_part)
            grad = (gain_ref[:, cols(h)] * scaled - value * pull).astype(BF16)
            grad_att[:, cols(h)] = grad
            first = dot(at(q_ref, 0, h), grad[:BLOCK], 0, 0)
            second = dot(at(q_ref, 1, h), grad[BLOCK:], 0, 0)
            inner_b[h] = second
            put_total(total_b, h, first + second)
        if c == CHUNKS - 1:
            for s in range(PLANE):
                total_b[c, s, piece : piece + 8] = gain_part
        backward.plane_out(c)

    def inside_grads(h):
        state = carried_state(earlier, h)
        for b in range(block_count):
            rows = slice(b * BLOCK, (b + 1) * BLOCK)
            grad = grad_att[rows, cols(h)]
            products = dot(grad, at(v_ref, b, h), 1, 1)
            grad_scores = jnp.where(causal, products, 0.0).astype(BF16)
            here = state + inner[h] if b == 1 else state
            value = dot(grad_scores, at(k_ref, b, h), 1, 0) + dot_wide(grad, here, 1)
            gq_ref[rows, cols(h)] = value.astype(BF16)
            key = dot(grad_scores, at(q_ref, b, h), 0, 0)
            val = dot(scores[rows, cols(h)], grad, 0, 0)
            if b == 0:
                key = key + dot_wide(at(v_ref, b, h), inner_b[h], 1)
                val = val + dot_wide(at(k_ref, b, h), inner_b[h], 0)
            gk_part[rows, cols(h)] = key
            gv_part[rows, cols(h)] = val

    for h in range(head_count // 2):
        inside_grads(h)
    for c in range(CHUNKS):
        backward.near_out(c)
    for h in range(head_count // 2, 3 * head_count // 4):
        inside_grads(h)
    for c in range(CHUNKS):
        backward.far_out(c)
    for h in range(3 * head_count // 4, head_count):
        inside_grads(h)
    for c in range(CHUNKS):
        backward.plane_back(c)
    last = CHUNKS - 1
    gain_rows = slice(piece, piece + 8)
    whole_gain = backward.before[last][gain_rows] + step_b[last, gain_rows]
    for i in range(len(FAR)):
        whole_gain = whole_gain + far_b[last, i, gain_rows]
    for h in range(head_count):
        gg_ref[:, cols(h)] = whole_gain[h : h + 1]
    for c in range(CHUNKS):
        backward.landed(c)
        for h in of_chunk(c):
            after = carried_state(later, h)
            key = gk_part[:, cols(h)] + dot_wide(v_ref[:, cols(h)], after, 1)
            gk_ref[:, cols(h)] = key.astype(BF16)
            val = gv_part[:, cols(h)] + dot_wide(k_ref[:, cols(h)], after, 0)
            gv_ref[:, cols(h)] = val.astype(BF16)
    for ref, sem in unsent:
        bytes_of(ref, sem)


def write_out(a_ref, b_ref, c_ref, d_ref, a_hbm, b_hbm, c_hbm, d_hbm, sem):
    copies = []
    pairs = ((a_ref, a_hbm), (b_ref, b_hbm), (c_ref, c_hbm), (d_ref, d_hbm))
    for i, (source, target) in enumerate(pairs):
        copies.append(pltpu.make_async_copy(source, target, sem.at[i]))
        copies[-1].start()
    for copy in copies:
        copy.wait()


def local(z_count, queries, key_vectors, value_vectors, out_grad, norm_gain):
    tokens, features = queries.shape
    head_count = features // DH
    block_count = tokens // BLOCK
    y_count = lax.axis_size("head")
    piece = head_count // CHUNKS * DH // PLANE
    like = jax.ShapeDtypeStruct((tokens, features), BF16)
    shapes = (like, like, like, jax.ShapeDtypeStruct((1, features), F32))
    vmem = pl.BlockSpec(memory_space=pltpu.VMEM)
    hbm = pl.BlockSpec(memory_space=pltpu.HBM)

    def scan_scratch(rows):
        return [
            pltpu.VMEM((CHUNKS, PLANE, rows, DH), F32),
            pltpu.VMEM((CHUNKS, PLANE, rows, DH), F32),
            pltpu.VMEM((CHUNKS, rows, DH), F32),
            pltpu.VMEM((CHUNKS, len(NEAR), rows, DH), F32),
            pltpu.VMEM((CHUNKS, len(FAR), rows, DH), F32),
            pltpu.VMEM((CHUNKS, len(FAR), rows, DH), F32),
            pltpu.VMEM((CHUNKS, PLANE, piece, DH), F32),
        ]

    operands = (queries, key_vectors, value_vectors, out_grad, norm_gain.reshape(1, features))
    results = pl.pallas_call(
        functools.partial(kernel, z_count, y_count, head_count, block_count),
        out_shape=shapes,
        in_specs=[hbm] * 5,
        out_specs=(vmem,) * 4,
        scratch_shapes=[
            *[pltpu.VMEM((tokens, features), BF16)] * 4,
            pltpu.VMEM((1, features), F32),
            pltpu.VMEM((head_count, DH, DH), F32),
            pltpu.VMEM((head_count, DH, DH), F32),
            pltpu.VMEM((tokens, features), F32),
            pltpu.VMEM((tokens, features), BF16),
            pltpu.VMEM((tokens, features), BF16),
            pltpu.VMEM((tokens, features), F32),
            pltpu.VMEM((tokens, features), F32),
            pltpu.VMEM((CHUNKS, PLANE, piece, DH), F32),
            pltpu.VMEM((CHUNKS, PLANE, piece, DH), F32),
            *scan_scratch(piece),
            *scan_scratch(piece + 8),
            pltpu.VMEM((y_count, 2, tokens), F32),
            *[pltpu.SemaphoreType.DMA((CHUNKS, 4))] * 4,
            pltpu.SemaphoreType.DMA,
            pltpu.SemaphoreType.DMA,
            pltpu.SemaphoreType.DMA((5,)),
        ],
        compiler_params=pltpu.CompilerParams(
            collective_id=0, has_side_effects=True, vmem_limit_bytes=32 * 1024 * 1024
        ),
        name="linear_attention_backward",
    )(*[pltpu.with_memory_space_constraint(x, pltpu.HBM) for x in operands])
    outs = pl.pallas_call(
        write_out,
        out_shape=shapes,
        in_specs=[vmem] * 4,
        out_specs=(hbm,) * 4,
        scratch_shapes=[pltpu.SemaphoreType.DMA((4,))],
        name="write_out",
    )(*[pltpu.with_memory_space_constraint(x, pltpu.VMEM) for x in results])
    return outs[0], outs[1], outs[2], outs[3].reshape(features)


def solution(mesh):
    in_specs = (P("seq", "head"), P("seq", "head"), P("seq", "head"), P("seq", "head"), P("head"))
    out_specs = (P("seq", "head"), P("seq", "head"), P("seq", "head"), P("head"))
    body = functools.partial(local, mesh.shape["seq"] // PLANE)
    return jax.shard_map(body, mesh=mesh, in_specs=in_specs, out_specs=out_specs, check_vma=False)
```

```python
import functools

import jax
import jax.numpy as jnp
from jax import lax
from jax.experimental import pallas as pl
from jax.experimental.pallas import tpu as pltpu
from jax.sharding import PartitionSpec as P

DH = 128
BLOCK = 128
PLANE = 8
NEAR = (2, -2, 1, -1)
FAR = ((4, (-2, -1, 0, 1)), (-4, (-1, 0, 1)))
EPSILON = 1e-06
CHUNKS = 4
MESH = pl.DeviceIdType.MESH
F32 = jnp.float32
BF16 = jnp.bfloat16


def dot(left, right, left_dim, right_dim):
    return lax.dot_general(
        left, right, (((left_dim,), (right_dim,)), ((), ())), preferred_element_type=F32
    )


def split(wide):
    high = wide.astype(BF16)
    low = (wide - high.astype(F32)).astype(BF16)
    return high, low


def dot_wide(left, wide, wide_dim):
    high, low = split(wide)
    return dot(left, high, 1, wide_dim) + dot(left, low, 1, wide_dim)


def kernel(
    z_count, y_count, head_count, block_count,
    q_hbm, k_hbm, v_hbm, g_hbm, gain_hbm,
    gq_ref, gk_ref, gv_ref, gg_ref,
    q_ref, k_ref, v_ref, g_ref, gain_ref,
    inner, inner_b, att, scores, grad_att, gk_part, gv_part, earlier, later,
    total_f, plane_f, step_f, near_f, window_f, far_f, stage_f,
    total_b, plane_b, step_b, near_b, window_b, far_b, stage_b,
    sums,
    f_send, f_recv, b_send, b_recv, h_send, h_recv, load_sem,
):
    loads = {}
    pairs = ((k_hbm, k_ref), (v_hbm, v_ref), (q_hbm, q_ref), (g_hbm, g_ref), (gain_hbm, gain_ref))
    for i, (source, target) in enumerate(pairs):
        loads[i] = pltpu.make_async_copy(source, target, load_sem.at[i])
        if i < 2:
            loads[i].start()

    seq = lax.axis_index("seq")
    y = lax.axis_index("head")
    z = lax.div(seq, PLANE)
    p = lax.rem(seq, PLANE)
    heads_each = head_count // CHUNKS
    piece = heads_each * DH // PLANE
    model_width = y_count * head_count * DH

    def in_plane(offset):
        return lax.rem(p + offset, PLANE)

    def in_column(offset):
        return lax.rem(z + offset, z_count)

    def seq_of(at_z, at_p):
        return at_z * PLANE + at_p

    hops = NEAR + tuple(d for d, _ in FAR)
    barrier = pltpu.get_barrier_semaphore()
    farthest_first = (4, 3, 5, 2, 6, 1, 7)
    for d in sorted(hops, key=abs, reverse=True):
        to = seq_of(in_column(d % z_count), p)
        pl.semaphore_signal(barrier, inc=1, device_id=(to, y), device_id_type=MESH)
    for k in farthest_first:
        to = lax.rem(y + k, y_count)
        pl.semaphore_signal(barrier, inc=1, device_id=(seq, to), device_id_type=MESH)
    for k in farthest_first:
        pl.semaphore_signal(barrier, inc=1, device_id=(seq_of(z, in_plane(k)), y), device_id_type=MESH)

    for i in range(2, len(pairs)):
        loads[i].start()
    unsent = []

    def remote(source, target, send, recv, seq_to, y_to):
        copy = pltpu.make_async_remote_copy(
            src_ref=source, dst_ref=target, send_sem=send, recv_sem=recv,
            device_id=(seq_to, y_to), device_id_type=MESH,
        )
        copy.start()

    def bytes_of(ref, sem):
        pltpu.make_async_copy(ref, ref, sem).wait()

    def flying(ref, send, recv):
        unsent.append((ref, send))
        return ref, recv

    row = lax.broadcasted_iota(jnp.int32, (BLOCK, BLOCK), 0)
    col = lax.broadcasted_iota(jnp.int32, (BLOCK, BLOCK), 1)
    causal = row >= col
    part_rows = DH // PLANE * heads_each
    halves = DH // part_rows if part_rows < DH else 1

    def at(ref, b, h):
        return ref[b * BLOCK : (b + 1) * BLOCK, h * DH : (h + 1) * DH]

    def cols(h):
        return slice(h * DH, (h + 1) * DH)

    def put_total(total, h, value):
        c, place = divmod(h, heads_each)
        for i in range(halves):
            total[c, place * halves + i, 0:piece] = value[i * piece : (i + 1) * piece]

    def carried_state(ref, h):
        c, place = divmod(h, heads_each)
        return jnp.concatenate([ref[c, place * halves + i] for i in range(halves)], axis=0)

    class Scan:
        def __init__(self, refs, target, sems, reverse):
            self.total, self.plane, self.step, self.near, self.window, self.far, self.stage = refs
            self.target = target
            self.send, self.recv = sems
            self.reverse = reverse
            self.flying = {}
            self.before = {}

        def fly(self, c, phase, ref):
            self.flying[c] = flying(ref, self.send.at[c, phase], self.recv.at[c, phase])

        def rows(self, c):
            return piece + 8 if self.reverse and c == CHUNKS - 1 else piece

        def around(self, c, place, n):
            if place == 0:
                return self.step[c, 0:n]
            return self.near[c, NEAR.index(-place), 0:n]

        def collect(self, c, distance, places):
            n = self.rows(c)
            here = z_count - 1 - z if self.reverse else z
            target = lax.rem(here + distance % z_count, z_count)
            state = None
            for place in places:
                behind = (distance - place) % z_count
                value = self.around(c, place, n)
                kept = jnp.where(target >= behind, value[:piece], 0.0)
                state = kept if state is None else state + kept
            if n == piece:
                return state
            gain = self.around(c, places[0], n)[piece:]
            for place in places[1:]:
                gain = gain + self.around(c, place, n)[piece:]
            return jnp.concatenate([state, gain], axis=0)

        def plane_out(self, c):
            n = self.rows(c)
            for k in (1, 7, 2, 6, 3, 5, 4):
                to = in_plane(k)
                remote(
                    self.total.at[c, to, 0:n], self.plane.at[c, p, 0:n],
                    self.send.at[c, 0], self.recv.at[c, 0], seq_of(z, to), y,
                )
            self.fly(c, 0, self.plane.at[c, 0 : PLANE - 1, 0:n])
            self.plane[c, p] = self.total[c, p]

        def column_out(self, c, phase, distance, source, target):
            to = in_column((-distance if self.reverse else distance) % z_count)
            remote(source, target, self.send.at[c, phase], self.recv.at[c, phase], seq_of(to, p), y)

        def near_out(self, c):
            n = self.rows(c)
            bytes_of(*self.flying[c])
            value = self.plane[c, 0, 0:n]
            for s in range(1, PLANE):
                value = value + self.plane[c, s, 0:n]
            self.step[c, 0:n] = value
            for i, d in enumerate(NEAR):
                self.column_out(c, 1, d, self.step.at[c, 0:n], self.near.at[c, i, 0:n])
            self.fly(c, 1, self.near.at[c, :, 0:n])

        def far_out(self, c):
            n = self.rows(c)
            bytes_of(*self.flying[c])
            for i, (d, places) in enumerate(FAR):
                self.window[c, i, 0:n] = self.collect(c, d, places)
                self.column_out(c, 2, d, self.window.at[c, i, 0:n], self.far.at[c, i, 0:n])
            self.fly(c, 2, self.far.at[c, :, 0:n])
            self.before[c] = self.collect(c, 0, tuple(-d for d in NEAR))

        def plane_back(self, c):
            bytes_of(*self.flying[c])
            value = self.before[c][:piece]
            for i in range(len(FAR)):
                value = value + self.far[c, i, 0:piece]
            order = range(PLANE - 1, -1, -1) if self.reverse else range(PLANE)
            for s in order:
                self.stage[c, s] = value
                value = value + self.plane[c, s, 0:piece]
            for k in (1, 7, 2, 6, 3, 5, 4):
                to = in_plane(k)
                remote(
                    self.stage.at[c, to], self.target.at[c, p],
                    self.send.at[c, 3], self.recv.at[c, 3], seq_of(z, to), y,
                )
            self.fly(c, 3, self.target.at[c, 0 : PLANE - 1])
            self.target[c, p] = self.stage[c, p]

        def landed(self, c):
            bytes_of(*self.flying[c])

    forward = Scan(
        (total_f, plane_f, step_f, near_f, window_f, far_f, stage_f), earlier,
        (f_send, f_recv), False,
    )
    backward = Scan(
        (total_b, plane_b, step_b, near_b, window_b, far_b, stage_b), later,
        (b_send, b_recv), True,
    )

    def of_chunk(c):
        return range(c * heads_each, (c + 1) * heads_each)

    loads[0].wait()
    loads[1].wait()
    for c in range(CHUNKS):
        for h in of_chunk(c):
            first = dot(at(k_ref, 0, h), at(v_ref, 0, h), 0, 0)
            second = dot(at(k_ref, 1, h), at(v_ref, 1, h), 0, 0)
            inner[h] = first
            put_total(total_f, h, first + second)
        if c == 0:
            pl.semaphore_wait(barrier, PLANE - 1 + len(hops) + y_count - 1)
        forward.plane_out(c)

    def inside(h):
        for b in range(block_count):
            products = dot(at(q_ref, b, h), at(k_ref, b, h), 1, 1)
            kept = jnp.where(causal, products, 0.0).astype(BF16)
            scores[b * BLOCK : (b + 1) * BLOCK, cols(h)] = kept
            value = dot(kept, at(v_ref, b, h), 1, 0)
            if b == 1:
                value = value + dot_wide(at(q_ref, b, h), inner[h], 0)
            att[b * BLOCK : (b + 1) * BLOCK, cols(h)] = value

    loads[2].wait()
    for h in range(head_count // 2):
        inside(h)
    for c in range(CHUNKS):
        forward.near_out(c)
    for h in range(head_count // 2, head_count):
        inside(h)
    for c in range(CHUNKS):
        forward.far_out(c)
    for c in range(CHUNKS):
        forward.plane_back(c)
    loads[3].wait()
    loads[4].wait()

    tokens = block_count * BLOCK
    squares = jnp.zeros((tokens, DH), F32)
    weighted = jnp.zeros((tokens, DH), F32)
    for c in range(CHUNKS):
        forward.landed(c)
        for h in of_chunk(c):
            value = att[:, cols(h)] + dot_wide(q_ref[:, cols(h)], carried_state(earlier, h), 0)
            att[:, cols(h)] = value
            squares = squares + value * value
            weighted = weighted + gain_ref[:, cols(h)] * g_ref[:, cols(h)].astype(F32) * value
    square_row = jnp.sum(squares.T, axis=0, keepdims=True)
    weighted_row = jnp.sum(weighted.T, axis=0, keepdims=True)
    sums[0, 0:1] = square_row
    sums[0, 1:2] = weighted_row
    for k in farthest_first:
        remote(sums.at[0], sums.at[k], h_send, h_recv, seq, lax.rem(y + k, y_count))
    bytes_of(*flying(sums.at[1:y_count], h_send, h_recv))
    whole = sums[0]
    for k in range(1, y_count):
        whole = whole + sums[k]
    inverse_row = 1.0 / jnp.sqrt(whole[0:1] / model_width + EPSILON)
    pull_row = inverse_row * inverse_row * inverse_row * whole[1:2] / model_width
    inverse = jnp.broadcast_to(inverse_row, (DH, tokens)).T
    pull = jnp.broadcast_to(pull_row, (DH, tokens)).T

    gain_line = lax.broadcasted_iota(jnp.int32, (8, DH), 0)
    gain_part = jnp.zeros((8, DH), F32)
    for c in range(CHUNKS):
        for h in of_chunk(c):
            value = att[:, cols(h)]
            scaled = g_ref[:, cols(h)].astype(F32) * inverse
            gain_sum = jnp.sum(scaled * value, axis=0, keepdims=True)
            gain_part = jnp.where(gain_line == h, gain_sum, gain_part)
            grad = (gain_ref[:, cols(h)] * scaled - value * pull).astype(BF16)
            grad_att[:, cols(h)] = grad
            first = dot(at(q_ref, 0, h), grad[:BLOCK], 0, 0)
            second = dot(at(q_ref, 1, h), grad[BLOCK:], 0, 0)
            inner_b[h] = second
            put_total(total_b, h, first + second)
        if c == CHUNKS - 1:
            for s in range(PLANE):
                total_b[c, s, piece : piece + 8] = gain_part
        backward.plane_out(c)

    def inside_grads(h):
        state = carried_state(earlier, h)
        for b in range(block_count):
            rows = slice(b * BLOCK, (b + 1) * BLOCK)
            grad = grad_att[rows, cols(h)]
            products = dot(grad, at(v_ref, b, h), 1, 1)
            grad_scores = jnp.where(causal, products, 0.0).astype(BF16)
            here = state + inner[h] if b == 1 else state
            value = dot(grad_scores, at(k_ref, b, h), 1, 0) + dot_wide(grad, here, 1)
            gq_ref[rows, cols(h)] = value.astype(BF16)
            key = dot(grad_scores, at(q_ref, b, h), 0, 0)
            val = dot(scores[rows, cols(h)], grad, 0, 0)
            if b == 0:
                key = key + dot_wide(at(v_ref, b, h), inner_b[h], 1)
                val = val + dot_wide(at(k_ref, b, h), inner_b[h], 0)
            gk_part[rows, cols(h)] = key
            gv_part[rows, cols(h)] = val

    for h in range(head_count // 2):
        inside_grads(h)
    for c in range(CHUNKS):
        backward.near_out(c)
    for h in range(head_count // 2, 3 * head_count // 4):
        inside_grads(h)
    for c in range(CHUNKS):
        backward.far_out(c)
    for h in range(3 * head_count // 4, head_count):
        inside_grads(h)
    for c in range(CHUNKS):
        backward.plane_back(c)
    last = CHUNKS - 1
    gain_rows = slice(piece, piece + 8)
    whole_gain = backward.before[last][gain_rows] + step_b[last, gain_rows]
    for i in range(len(FAR)):
        whole_gain = whole_gain + far_b[last, i, gain_rows]
    for h in range(head_count):
        gg_ref[:, cols(h)] = whole_gain[h : h + 1]
    for c in range(CHUNKS):
        backward.landed(c)
        for h in of_chunk(c):
            after = carried_state(later, h)
            key = gk_part[:, cols(h)] + dot_wide(v_ref[:, cols(h)], after, 1)
            gk_ref[:, cols(h)] = key.astype(BF16)
            val = gv_part[:, cols(h)] + dot_wide(k_ref[:, cols(h)], after, 0)
            gv_ref[:, cols(h)] = val.astype(BF16)
    for ref, sem in unsent:
        bytes_of(ref, sem)


def write_out(a_ref, b_ref, c_ref, d_ref, a_hbm, b_hbm, c_hbm, d_hbm, sem):
    copies = []
    pairs = ((a_ref, a_hbm), (b_ref, b_hbm), (c_ref, c_hbm), (d_ref, d_hbm))
    for i, (source, target) in enumerate(pairs):
        copies.append(pltpu.make_async_copy(source, target, sem.at[i]))
        copies[-1].start()
    for copy in copies:
        copy.wait()


def local(z_count, queries, key_vectors, value_vectors, out_grad, norm_gain):
    tokens, features = queries.shape
    head_count = features // DH
    block_count = tokens // BLOCK
    y_count = lax.axis_size("head")
    piece = head_count // CHUNKS * DH // PLANE
    like = jax.ShapeDtypeStruct((tokens, features), BF16)
    shapes = (like, like, like, jax.ShapeDtypeStruct((1, features), F32))
    vmem = pl.BlockSpec(memory_space=pltpu.VMEM)
    hbm = pl.BlockSpec(memory_space=pltpu.HBM)

    def scan_scratch(rows):
        return [
            pltpu.VMEM((CHUNKS, PLANE, rows, DH), F32),
            pltpu.VMEM((CHUNKS, PLANE, rows, DH), F32),
            pltpu.VMEM((CHUNKS, rows, DH), F32),
            pltpu.VMEM((CHUNKS, len(NEAR), rows, DH), F32),
            pltpu.VMEM((CHUNKS, len(FAR), rows, DH), F32),
            pltpu.VMEM((CHUNKS, len(FAR), rows, DH), F32),
            pltpu.VMEM((CHUNKS, PLANE, piece, DH), F32),
        ]

    operands = (queries, key_vectors, value_vectors, out_grad, norm_gain.reshape(1, features))
    results = pl.pallas_call(
        functools.partial(kernel, z_count, y_count, head_count, block_count),
        out_shape=shapes,
        in_specs=[hbm] * 5,
        out_specs=(vmem,) * 4,
        scratch_shapes=[
            *[pltpu.VMEM((tokens, features), BF16)] * 4,
            pltpu.VMEM((1, features), F32),
            pltpu.VMEM((head_count, DH, DH), F32),
            pltpu.VMEM((head_count, DH, DH), F32),
            pltpu.VMEM((tokens, features), F32),
            pltpu.VMEM((tokens, features), BF16),
            pltpu.VMEM((tokens, features), BF16),
            pltpu.VMEM((tokens, features), F32),
            pltpu.VMEM((tokens, features), F32),
            pltpu.VMEM((CHUNKS, PLANE, piece, DH), F32),
            pltpu.VMEM((CHUNKS, PLANE, piece, DH), F32),
            *scan_scratch(piece),
            *scan_scratch(piece + 8),
            pltpu.VMEM((y_count, 2, tokens), F32),
            *[pltpu.SemaphoreType.DMA((CHUNKS, 4))] * 4,
            pltpu.SemaphoreType.DMA,
            pltpu.SemaphoreType.DMA,
            pltpu.SemaphoreType.DMA((5,)),
        ],
        compiler_params=pltpu.CompilerParams(
            collective_id=0, has_side_effects=True, vmem_limit_bytes=32 * 1024 * 1024
        ),
        name="linear_attention_backward",
    )(*[pltpu.with_memory_space_constraint(x, pltpu.HBM) for x in operands])
    outs = pl.pallas_call(
        write_out,
        out_shape=shapes,
        in_specs=[vmem] * 4,
        out_specs=(hbm,) * 4,
        scratch_shapes=[pltpu.SemaphoreType.DMA((4,))],
        name="write_out",
    )(*[pltpu.with_memory_space_constraint(x, pltpu.VMEM) for x in results])
    return outs[0], outs[1], outs[2], outs[3].reshape(features)


def solution(mesh):
    in_specs = (P("seq", "head"), P("seq", "head"), P("seq", "head"), P("seq", "head"), P("head"))
    out_specs = (P("seq", "head"), P("seq", "head"), P("seq", "head"), P("head"))
    body = functools.partial(local, mesh.shape["seq"] // PLANE)
    return jax.shard_map(body, mesh=mesh, in_specs=in_specs, out_specs=out_specs, check_vma=False)
```
